32 devices in a mesh: video: 2 (over x), row: 16 (over z, y, core).
Axes of the slice: x: 2, y: 2, z: 4, core: 2. Of those that a mesh axis runs over, the one named last changes fastest.
Arguments:
- stream: bfloat16 [8, 16, 32, 1536], P('video', 'row'), parts along dimension 0, may hold values from -0.8984375 to 0.8984375
- query: bfloat16 [8, 16, 32, 1536], P('video', 'row'), parts along dimension 0, may hold values from -30 to 30
- key: bfloat16 [8, 16, 32, 1536], P('video', 'row'), parts along dimension 0, may hold values from -6 to 6
- value: bfloat16 [8, 16, 32, 1536], P('video', 'row'), parts along dimension 0, may hold values from -6 to 6
- attn_gate: float32 [3072], P('video'), parts along dimension 0, may hold values from 1 to 3
- shift_mod: float32 [3072], P('video'), parts along dimension 0, may hold values from -3 to 3
- scale_mod: float32 [3072], P('video'), parts along dimension 0, may hold values from -3 to 3
- head_weight: bfloat16 [1536, 64], replicated, may hold values from -0.15625 to 0.15625
- head_bias: float32 [64], replicated, may hold values from -3 to 3
- latent_mean: float32 [16], replicated, may hold values from -3 to 3
- latent_std: float32 [16], replicated, may hold values from 0.5 to 2
- conv_in_weight: bfloat16 [3, 3, 3, 16, 384], replicated, may hold values from -0.3125 to 0.3125
- conv_in_bias: float32 [384], replicated, may hold values from -2 to 2
- norm_gain: float32 [384], replicated, may hold values from 0.5 to 1.5
- conv_weight: bfloat16 [3, 3, 3, 384, 384], replicated, may hold values from -0.0625 to 0.0625
- conv_bias: float32 [384], replicated, may hold values from -2 to 2
Outputs:
- decoded: bfloat16 [8, 32, 64, 384], P('video', 'row'), parts along dimension 0
The draws below stay inside these ranges and needn't reach their ends.
There are 2 independent parts, one for each index of `video`. The reference program is written for one: setup_inputs(seed, part) draws one part's arguments, and reference() takes and returns one part's arrays. A program takes and returns all parts, laid end to end along the dimension named above; an argument that names none is the same for every part. Nothing has to cross between parts.
All inputs are finite; a program needn't handle non-finite values.
Results may differ from the reference program's by a relative error of at most 0.0069.
Values may be sent and summed in bfloat16 or wider, within the bound.
A program may use at most 128 MiB of HBM per device.

```python
import math
import jax
import jax.numpy as jnp
import numpy as np
from jax import lax

D = 1536
HEADS = 12
C = 384
LAT = 16
F = 4
W = 32
H = 16


def pair_draw(key):
    base_key = jax.random.fold_in(key, 4211)
    shape = (F, H, W, D)
    queries = jax.random.truncated_normal(jax.random.fold_in(base_key, 1), -6.0, 6.0, shape, jnp.float32)
    keys = jax.random.truncated_normal(jax.random.fold_in(base_key, 2), -6.0, 6.0, shape, jnp.float32)
    return (queries, keys)


def draw_query(key, part):
    return pair_draw(key)[0].astype(jnp.bfloat16)


def draw_key(key, part):
    return pair_draw(key)[1].astype(jnp.bfloat16)


def steps_of(stream_key, dims, shards, low, top_value):
    def one(dim, shards_of):
        steps = jax.random.uniform(jax.random.fold_in(jax.random.fold_in(stream_key, 6), dim), (shards_of,), jnp.float32, low / len(shards), top_value / len(shards))
        return jnp.repeat(jnp.exp(steps), dims[dim] // shards_of).reshape((-1,) + (1,) * (len(dims) - dim - 1))

    factor_of = one(*shards[0])
    for cut in shards[1:]:
        factor_of = factor_of * one(*cut)
    return factor_of


def gaussian(rng, dims, scale, reach, pieces=(), kind=jnp.bfloat16):
    loudness = steps_of(rng, dims, pieces, -0.22, 0.18) if pieces else 1.0
    result = jax.random.normal(rng, dims, jnp.float32) * scale * loudness
    return jnp.minimum(jnp.maximum(result, -reach), reach).astype(kind)


def setup_inputs(seed: int = 0, part: int = 0) -> dict:
    key_of = jax.random.split(jax.random.key(seed), 17)
    part_splits = jax.random.split(jax.random.fold_in(key_of[16], part), 17)
    stream = gaussian(part_splits[0], (F, H, W, D), 0.15, 0.8984375, ((1, 16),))
    query = draw_query(jax.random.fold_in(jax.random.fold_in(key_of[16], part), 71), part)
    key = draw_key(jax.random.fold_in(jax.random.fold_in(key_of[16], part), 71), part)
    value = gaussian(part_splits[3], (F, H, W, D), 1.0, 6.0, ((1, 16),))
    attn_gate = jnp.clip(jax.random.uniform(part_splits[4], (D,), jnp.float32, 1.0, 3.0), 1.0, 3.0)
    shift_mod = gaussian(part_splits[5], (D,), 0.5, 3.0, (), jnp.float32)
    scale_mod = gaussian(part_splits[6], (D,), 0.5, 3.0, (), jnp.float32)
    head_weight = gaussian(key_of[7], (D, 4 * LAT), D ** -0.5, 0.15625)
    head_bias = gaussian(key_of[8], (4 * LAT,), 0.5, 3.0, (), jnp.float32)
    latent_mean = gaussian(key_of[9], (LAT,), 0.5, 3.0, (), jnp.float32)
    latent_std = jnp.clip(jnp.exp(jax.random.uniform(key_of[10], (LAT,), jnp.float32, math.log(0.5), math.log(2.0))), 0.5, 2.0)
    conv_in_weight = gaussian(key_of[11], (3, 3, 3, LAT, C), (27 * LAT) ** -0.5, 0.3125)
    conv_in_bias = gaussian(key_of[12], (C,), 0.3, 2.0, (), jnp.float32)
    norm_gain = jnp.clip(jax.random.uniform(key_of[13], (C,), jnp.float32, 0.5, 1.5), 0.5, 1.5)
    conv_weight = gaussian(key_of[14], (3, 3, 3, C, C), (27 * C) ** -0.5, 0.0625)
    conv_bias = gaussian(key_of[15], (C,), 0.3, 2.0, (), jnp.float32)
    return {"stream": stream, "query": query, "key": key, "value": value, "attn_gate": attn_gate, "shift_mod": shift_mod, "scale_mod": scale_mod, "head_weight": head_weight, "head_bias": head_bias, "latent_mean": latent_mean, "latent_std": latent_std, "conv_in_weight": conv_in_weight, "conv_in_bias": conv_in_bias, "norm_gain": norm_gain, "conv_weight": conv_weight, "conv_bias": conv_bias}


def causal_conv(rows_padded, weight):
    frames, padded_rows, columns, in_width = rows_padded.shape
    out_rows = padded_rows - 2
    out_width = weight.shape[-1]
    padded = jnp.pad(rows_padded, ((2, 0), (0, 0), (1, 1), (0, 0)))
    summed = jnp.zeros((frames * out_rows * columns, out_width), jnp.float32)
    for a in range(3):
        for b in range(3):
            for e in range(3):
                slab = padded[a:a + frames, b:b + out_rows, e:e + columns].reshape(-1, in_width)
                summed = summed + jnp.dot(slab.astype(jnp.float32), weight[a, b, e].astype(jnp.float32), preferred_element_type=jnp.float32)
    return summed.reshape(frames, out_rows, columns, out_width)

def activate(hidden, gain):
    values = hidden.astype(jnp.float32)
    scaled = values * lax.rsqrt(lax.optimization_barrier(jnp.mean(values * values, axis=-1, keepdims=True)) + 1e-06) * gain
    return jax.nn.silu(scaled).astype(jnp.bfloat16)

def reference(stream, query, key, value, attn_gate, shift_mod, scale_mod, head_weight, head_bias, latent_mean, latent_std, conv_in_weight, conv_in_bias, norm_gain, conv_weight, conv_bias):
    frames, rows, columns, width = query.shape
    head_size = width // HEADS
    scaling = head_size ** (-0.5)
    queries = query.reshape(frames, rows, columns, HEADS, head_size)
    key_pad = jnp.pad(key, ((0, 0), (3, 3), (0, 0), (0, 0))).reshape(frames, rows + 6, columns, HEADS, head_size)
    value_pad = jnp.pad(value, ((0, 0), (3, 3), (0, 0), (0, 0))).reshape(frames, rows + 6, columns, HEADS, head_size)
    col_start = np.clip(np.arange(columns) - 3, 0, columns - 7)
    col_index = np.arange(columns)
    band = jnp.asarray((col_index[None, :] >= col_start[:, None]) & (col_index[None, :] < col_start[:, None] + 7))
    offsets = jnp.arange(7, dtype=jnp.int32)

    def one_row(pair):
        frame_idx = pair[0]
        row_idx = pair[1]
        start = jnp.clip(frame_idx - 1, 0, frames - 3).astype(jnp.int32)
        zero = jnp.zeros((), jnp.int32)
        keys = lax.dynamic_slice(key_pad, (start, row_idx, zero, zero, zero), (3, 7, columns, HEADS, head_size))
        values = lax.dynamic_slice(value_pad, (start, row_idx, zero, zero, zero), (3, 7, columns, HEADS, head_size))
        query_row = lax.dynamic_slice(queries, (frame_idx, row_idx, zero, zero, zero), (1, 1, columns, HEADS, head_size))[0, 0]
        raw = jnp.einsum('whd,arvhd->arwhv', query_row.astype(jnp.float32), keys.astype(jnp.float32)) * scaling
        source_row = row_idx + offsets - 3
        rows_ok = (source_row >= 0) & (source_row < rows)
        allowed = rows_ok[None, :, None, None, None] & band[None, None, :, None, :]
        masked = jnp.where(allowed, raw, -jnp.inf)
        peak = lax.optimization_barrier(jnp.max(masked, axis=(0, 1, 4), keepdims=True))
        exp_terms = jnp.exp(masked - peak)
        attn_probs = (exp_terms / lax.optimization_barrier(jnp.sum(exp_terms, axis=(0, 1, 4), keepdims=True))).astype(jnp.bfloat16)
        attn_probs = lax.optimization_barrier(attn_probs)
        attended = jnp.einsum('arwhv,arvhd->whd', attn_probs.astype(jnp.float32), values.astype(jnp.float32))
        return attended.reshape(columns, width).astype(jnp.bfloat16)
    frame_ids = jnp.repeat(jnp.arange(frames, dtype=jnp.int32), rows)
    row_ids = jnp.tile(jnp.arange(rows, dtype=jnp.int32), frames)
    attn = lax.map(one_row, jnp.stack([frame_ids, row_ids], axis=1)).reshape(frames, rows, columns, width)
    attn = lax.optimization_barrier(attn)
    resid = stream.astype(jnp.float32) + attn_gate * attn.astype(jnp.float32)
    center = resid - lax.optimization_barrier(jnp.mean(resid, axis=-1, keepdims=True))
    spread = lax.optimization_barrier(jnp.mean(center * center, axis=-1, keepdims=True))
    normed = (center * lax.rsqrt(spread + 1e-06) * (1.0 + scale_mod) + shift_mod).astype(jnp.bfloat16)
    patch = jnp.dot(normed.reshape(-1, width), head_weight, preferred_element_type=jnp.float32) + head_bias
    patch = patch.reshape(frames, rows, columns, 2, 2, LAT).transpose(0, 1, 3, 2, 4, 5).reshape(frames, 2 * rows, 2 * columns, LAT)
    latent = (patch * latent_std + latent_mean).astype(jnp.bfloat16)
    latent_pad = jnp.pad(latent, ((0, 0), (1, 1), (0, 0), (0, 0)))
    hidden = (causal_conv(latent_pad, conv_in_weight) + conv_in_bias).astype(jnp.bfloat16)
    hidden = lax.optimization_barrier(hidden)
    act = activate(hidden, norm_gain)
    act_pad = jnp.pad(act, ((0, 0), (1, 1), (0, 0), (0, 0)))
    mixed = causal_conv(act_pad, conv_weight)
    return (hidden.astype(jnp.float32) + mixed + conv_bias).astype(jnp.bfloat16)
```

```python
import functools

import jax
import jax.numpy as jnp
from jax import lax
from jax.experimental import pallas as pl
from jax.experimental.pallas import tpu as pltpu
from jax.sharding import PartitionSpec as P

HEADS = 12
LAT = 16
GROUP = 4
HPD = HEADS // GROUP
HD = 128
FR = 4
COLS = 32
TOK = FR * COLS
ROWS_EXT = GROUP + 6
KEYS = FR * 7 * COLS
C = 384
NEG = -1e30


def attend_kernel(
    n_rows,
    stream_ref,
    q_ref,
    k_ref,
    v_ref,
    mods_ref,
    hw_ref,
    small_ref,
    out_ref,
    qb,
    kb,
    vb,
    ob,
    attn,
    bias,
    gbuf,
    own_sem,
    s1,
    r1,
    s2,
    r2,
    s3,
    r3,
    s4,
    r4,
):
    row = lax.axis_index("row")
    g = row // GROUP
    j = row % GROUP
    groups = n_rows // GROUP
    has_up = g > 0
    has_down = g < groups - 1
    first = row == 0
    last = row == n_rows - 1

    def head_cols(p, h):
        return pl.ds(pl.multiple_of((p * HPD + h) * HD, HD), HD)

    srcs = (k_ref, v_ref, q_ref)

    def level_dst(x, h, idx):
        if x == 2:
            return qb.at[h, idx]
        return (kb, vb)[x].at[h, :, idx + 3]

    own = []
    for h in range(HPD):
        for x in range(3):
            cp = pltpu.make_async_copy(
                srcs[x].at[:, :, head_cols(j, h)], level_dst(x, h, j), own_sem.at[x, h]
            )
            cp.start()
            own.append(cp)

    barrier = pltpu.get_barrier_semaphore()
    for d in range(1, GROUP):
        pl.semaphore_signal(barrier, inc=1, device_id={"row": g * GROUP + (j + d) % GROUP})

    @pl.when(has_up)
    def _():
        pl.semaphore_signal(barrier, inc=1, device_id={"row": row - GROUP})

    @pl.when(has_down)
    def _():
        pl.semaphore_signal(barrier, inc=1, device_id={"row": row + GROUP})

    cross_up = jnp.logical_and(j == 0, has_up)
    cross_down = jnp.logical_and(j == GROUP - 1, has_down)

    @pl.when(cross_up)
    def _():
        pl.semaphore_signal(barrier, inc=1, device_id={"row": row - 1})

    @pl.when(cross_down)
    def _():
        pl.semaphore_signal(barrier, inc=1, device_id={"row": row + 1})

    one = jnp.int32(1)
    zero = jnp.int32(0)
    expected = (
        3
        + jnp.where(has_up, one, zero)
        + jnp.where(has_down, one, zero)
        + jnp.where(cross_up, one, zero)
        + jnp.where(cross_down, one, zero)
    )
    pl.semaphore_wait(barrier, expected)

    def level_copy(x, h, d):
        p = (j + d) % GROUP
        return pltpu.make_async_remote_copy(
            src_ref=srcs[x].at[:, :, head_cols(p, h)],
            dst_ref=level_dst(x, h, j),
            send_sem=s1.at[x, h, d - 1],
            recv_sem=r1.at[x, h, d - 1],
            device_id={"row": g * GROUP + p},
        )

    for h in range(HPD):
        for x in range(2):
            for d in (2, 1, 3):
                level_copy(x, h, d).start()
    for h in range(HPD):
        for d in (2, 1, 3):
            level_copy(2, h, d).start()

    def edge_copy(x, h, up):
        buf = (kb, vb)[x]
        if up:
            src, dst, dev = buf.at[h, :, pl.ds(3, 3)], buf.at[h, :, pl.ds(7, 3)], row - GROUP
        else:
            src, dst, dev = buf.at[h, :, pl.ds(4, 3)], buf.at[h, :, pl.ds(0, 3)], row + GROUP
        way = 0 if up else 1
        return pltpu.make_async_remote_copy(
            src_ref=src,
            dst_ref=dst,
            send_sem=s2.at[x, h, way],
            recv_sem=r2.at[x, h, way],
            device_id={"row": dev},
        )

    tok_i = lax.broadcasted_iota(jnp.int32, (TOK, KEYS), 0)
    key_i = lax.broadcasted_iota(jnp.int32, (TOK, KEYS), 1)
    t = tok_i >> 5
    w = tok_i & 31
    span = 7 * COLS
    f = (
        jnp.where(key_i >= span, 1, 0)
        + jnp.where(key_i >= 2 * span, 1, 0)
        + jnp.where(key_i >= 3 * span, 1, 0)
    )
    fs = jnp.clip(t - 1, 0, FR - 3)
    cs = jnp.clip(w - 3, 0, COLS - 7)
    vcol = key_i & 31
    ok = (f >= fs) & (f < fs + 3) & (vcol >= cs) & (vcol < cs + 7)
    bias[...] = jnp.where(ok, 0.0, NEG)

    empty = jnp.zeros((HPD, FR, 3, COLS, HD), jnp.bfloat16)

    @pl.when(jnp.logical_not(has_up))
    def _():
        kb[:, :, 0:3] = empty
        vb[:, :, 0:3] = empty

    @pl.when(jnp.logical_not(has_down))
    def _():
        kb[:, :, 7:10] = empty
        vb[:, :, 7:10] = empty

    @pl.when(first)
    def _():
        gbuf[0] = jnp.zeros((TOK, 128), jnp.bfloat16)

    @pl.when(last)
    def _():
        gbuf[2] = jnp.zeros((TOK, 128), jnp.bfloat16)

    for cp in own:
        cp.wait()

    for h in range(HPD):
        for x in range(2):
            for d in range(1, GROUP):
                level_copy(x, h, d).wait_recv()

            @pl.when(has_up)
            def _():
                edge_copy(x, h, True).start()

            @pl.when(has_down)
            def _():
                edge_copy(x, h, False).start()

    key_row = lax.broadcasted_iota(jnp.int32, (1, KEYS), 1)
    fr = (
        jnp.where(key_row >= span, 1, 0)
        + jnp.where(key_row >= 2 * span, 1, 0)
        + jnp.where(key_row >= 3 * span, 1, 0)
    )
    rel_row = (key_row >> 5) - 7 * fr + (GROUP * g - 3)

    def out_copy(h, d):
        p = (j + d) % GROUP
        return pltpu.make_async_remote_copy(
            src_ref=ob.at[h, p],
            dst_ref=attn.at[j * HPD + h],
            send_sem=s3.at[h, d - 1],
            recv_sem=r3.at[h, d - 1],
            device_id={"row": g * GROUP + p},
        )

    for h in range(HPD):
        for d in range(1, GROUP):
            level_copy(2, h, d).wait_recv()
        for x in range(2):

            @pl.when(has_down)
            def _():
                edge_copy(x, h, True).wait_recv()

            @pl.when(has_up)
            def _():
                edge_copy(x, h, False).wait_recv()

        def one_row(i, carry):
            qm = qb[h, i].reshape(TOK, HD)
            km = kb[h, :, pl.ds(i, 7)].reshape(KEYS, HD)
            vm = vb[h, :, pl.ds(i, 7)].reshape(KEYS, HD)
            s = lax.dot_general(
                qm, km, (((1,), (1,)), ((), ())), preferred_element_type=jnp.float32
            )
            src_row = rel_row + i
            row_bias = jnp.where((src_row >= 0) & (src_row < n_rows), 0.0, NEG)
            s = s * (HD**-0.5) + (bias[...] + row_bias)
            m = jnp.max(s, axis=1, keepdims=True)
            e = jnp.exp(s - m)
            l = jnp.sum(e, axis=1, keepdims=True)
            pr = (e * (1.0 / l)).astype(jnp.bfloat16)
            o = jnp.dot(pr, vm, preferred_element_type=jnp.float32)
            ob[h, i] = o.astype(jnp.bfloat16)
            return carry

        lax.fori_loop(0, GROUP, one_row, 0)
        for d in (2, 1, 3):
            out_copy(h, d).start()
        attn[j * HPD + h] = ob[h, j]

    for h in range(HPD):
        for d in range(1, GROUP):
            out_copy(h, d).wait_recv()

    attn_all = jnp.concatenate([attn[c] for c in range(HEADS)], axis=-1)
    resid = stream_ref[...].astype(jnp.float32) + mods_ref[0:1, :] * attn_all.astype(jnp.float32)
    center = resid - jnp.mean(resid, axis=-1, keepdims=True)
    spread = jnp.mean(center * center, axis=-1, keepdims=True)
    normed = center * lax.rsqrt(spread + 1e-06) * (1.0 + mods_ref[2:3, :]) + mods_ref[1:2, :]
    patch = jnp.dot(
        normed.astype(jnp.bfloat16), hw_ref[...], preferred_element_type=jnp.float32
    )
    patch = patch + small_ref[0:1, :]
    latent = (patch * small_ref[1:2, :] + small_ref[2:3, :]).astype(jnp.bfloat16)

    dst_l = lax.broadcasted_iota(jnp.int32, (4 * LAT, 128), 1)
    src_l = lax.broadcasted_iota(jnp.int32, (4 * LAT, 128), 0)
    part = (dst_l >> 4) & 3
    want = ((dst_l >> 6) * 2 + (1 - (part & 1))) * LAT + (dst_l & 15)
    pick = jnp.where(src_l == want, 1.0, 0.0).astype(jnp.bfloat16)
    spreadout = jnp.dot(latent, pick, preferred_element_type=jnp.float32)
    lane = lax.broadcasted_iota(jnp.int32, (TOK, 128), 1)
    col = lax.broadcasted_iota(jnp.int32, (TOK, 128), 0) & 31
    lane_part = (lane >> 4) & 3
    before = jnp.where(col == 0, 0.0, pltpu.roll(spreadout, 1, 0))
    after = jnp.where(col == COLS - 1, 0.0, pltpu.roll(spreadout, TOK - 1, 0))
    cells = jnp.where(lane_part == 0, before, jnp.where(lane_part == 3, after, spreadout))
    gbuf[1] = cells.astype(jnp.bfloat16)

    def latent_copy(up):
        way = 0 if up else 1
        return pltpu.make_async_remote_copy(
            src_ref=gbuf.at[1],
            dst_ref=gbuf.at[2 if up else 0],
            send_sem=s4.at[way],
            recv_sem=r4.at[way],
            device_id={"row": row - 1 if up else row + 1},
        )

    @pl.when(jnp.logical_not(first))
    def _():
        latent_copy(True).start()

    @pl.when(jnp.logical_not(last))
    def _():
        latent_copy(False).start()

    for h in range(HPD):
        for x in range(3):
            for d in range(1, GROUP):
                level_copy(x, h, d).wait_send()
        for x in range(2):

            @pl.when(has_up)
            def _():
                edge_copy(x, h, True).wait_send()

            @pl.when(has_down)
            def _():
                edge_copy(x, h, False).wait_send()

        for d in range(1, GROUP):
            out_copy(h, d).wait_send()

    @pl.when(jnp.logical_not(first))
    def _():
        latent_copy(True).wait_send()
        latent_copy(False).wait_recv()

    @pl.when(jnp.logical_not(last))
    def _():
        latent_copy(False).wait_send()
        latent_copy(True).wait_recv()

    out_ref[...] = gbuf[...]


def decode_kernel(n_rows, cells_ref, cw_ref, vec_ref, w_ref, out_ref, w4, var, acc, wide):
    step = pl.program_id(0)
    a = step // 3
    b = step % 3

    @pl.when(step == 0)
    def _():
        row = lax.axis_index("row")
        w4[...] = jnp.zeros(w4.shape, jnp.bfloat16)
        for ab in range(9):
            w4[ab * 64 : ab * 64 + 48, 0:C] = cw_ref[ab]
            w4[ab * 64 + 16 : ab * 64 + 64, C : 2 * C] = cw_ref[ab]
        six = jnp.concatenate([cells_ref[i] for i in range(3)], axis=-1)
        col = lax.broadcasted_iota(jnp.int32, (TOK, C), 0) & 31
        zeros = jnp.zeros((2 * COLS, C), jnp.bfloat16)
        pad = jnp.zeros((2 * COLS, 192), jnp.bfloat16)
        for y in range(4):
            rows3 = six[:, y * 64 : y * 64 + 192]
            padded = jnp.concatenate([pad, rows3], axis=0)
            x = jnp.concatenate(
                [padded[i * COLS : i * COLS + TOK] for i in range(3)], axis=-1
            )
            h = jnp.dot(x, w4[...], preferred_element_type=jnp.float32)
            acts = []
            for q in range(2):
                hidden = (h[:, q * C : (q + 1) * C] + vec_ref[0:1, :]).astype(jnp.bfloat16)
                hidden = hidden.astype(jnp.float32)
                if y in (1, 2):
                    at = ((y - 1) * 2 + q) * TOK
                    acc[at : at + TOK, :] = hidden + vec_ref[2:3, :]
                ms = jnp.mean(hidden * hidden, axis=-1, keepdims=True)
                scaled = hidden * lax.rsqrt(ms + 1e-06) * vec_ref[1:2, :]
                act = scaled / (1.0 + jnp.exp(-scaled))
                if y == 0:
                    act = jnp.where(row > 0, act, 0.0)
                if y == 3:
                    act = jnp.where(row < n_rows - 1, act, 0.0)
                acts.append(act)
            before = jnp.where(col == 0, 0.0, pltpu.roll(acts[1], 1, 0))
            after = jnp.where(col == COLS - 1, 0.0, pltpu.roll(acts[0], TOK - 1, 0))
            for i, piece in enumerate((before, acts[0], acts[1], after)):
                var[i, y, 0 : 2 * COLS] = zeros
                var[i, y, 2 * COLS :] = piece.astype(jnp.bfloat16)

    start = pl.multiple_of(a * COLS, COLS)
    phases = []
    for y in range(2):
        taps = [var[i, y + b, pl.ds(start, TOK)] for i in range(4)]
        for q in range(2):
            phases.append(jnp.concatenate(taps[q : q + 3], axis=-1))
    lhs = jnp.concatenate(phases, axis=0)
    acc[...] += jnp.dot(lhs, w_ref[0], preferred_element_type=jnp.float32)

    @pl.when(step == 8)
    def _():
        for y in range(2):
            for q in range(2):
                for t in range(FR):
                    at = (y * 2 + q) * TOK + t * COLS
                    for c in range(3):
                        wide[t, y, c, pl.ds(q, COLS, stride=2), :] = acc[
                            at : at + COLS, c * 128 : (c + 1) * 128
                        ]
        for c in range(3):
            out_ref[:, :, :, c * 128 : (c + 1) * 128] = wide[:, :, c].astype(jnp.bfloat16)


def shards(
    n_rows,
    stream,
    query,
    key,
    value,
    attn_gate,
    shift_mod,
    scale_mod,
    head_weight,
    head_bias,
    latent_mean,
    latent_std,
    conv_in_weight,
    conv_in_bias,
    norm_gain,
    conv_weight,
    conv_bias,
):
    width = query.shape[-1]
    flat = (FR, COLS, width)
    mods = jnp.stack([attn_gate, shift_mod, scale_mod])
    small = jnp.stack([head_bias, jnp.tile(latent_std, 4), jnp.tile(latent_mean, 4)])
    vecs = jnp.stack([conv_in_bias, norm_gain, conv_bias])
    vmem = pl.BlockSpec(memory_space=pltpu.VMEM)
    anywhere = pl.BlockSpec(memory_space=pl.ANY)
    dma = pltpu.SemaphoreType.DMA
    bf = jnp.bfloat16
    cells = pl.pallas_call(
        functools.partial(attend_kernel, n_rows),
        out_shape=jax.ShapeDtypeStruct((3, TOK, 128), bf),
        in_specs=[vmem, anywhere, anywhere, anywhere, vmem, vmem, vmem],
        out_specs=vmem,
        scratch_shapes=[
            pltpu.VMEM((HPD, GROUP, FR, COLS, HD), bf),
            pltpu.VMEM((HPD, FR, ROWS_EXT, COLS, HD), bf),
            pltpu.VMEM((HPD, FR, ROWS_EXT, COLS, HD), bf),
            pltpu.VMEM((HPD, GROUP, TOK, HD), bf),
            pltpu.VMEM((HEADS, TOK, HD), bf),
            pltpu.VMEM((TOK, KEYS), jnp.float32),
            pltpu.VMEM((3, TOK, 128), bf),
            dma((3, HPD)),
            dma((3, HPD, 3)),
            dma((3, HPD, 3)),
            dma((2, HPD, 2)),
            dma((2, HPD, 2)),
            dma((HPD, 3)),
            dma((HPD, 3)),
            dma((2,)),
            dma((2,)),
        ],
        compiler_params=pltpu.CompilerParams(
            collective_id=0, has_side_effects=True, vmem_limit_bytes=24 << 20
        ),
        name="attend",
    )(
        stream.reshape(TOK, width),
        query.reshape(flat),
        key.reshape(flat),
        value.reshape(flat),
        mods,
        head_weight,
        small,
    )
    whole = lambda *shape: pl.BlockSpec(shape, lambda s: (0,) * len(shape))
    return pl.pallas_call(
        functools.partial(decode_kernel, n_rows),
        out_shape=jax.ShapeDtypeStruct((FR, 2, 2 * COLS, C), bf),
        grid=(9,),
        in_specs=[
            whole(3, TOK, 128),
            whole(9, 3 * LAT, C),
            whole(3, C),
            pl.BlockSpec((1, 3 * C, C), lambda s: (s, 0, 0)),
        ],
        out_specs=whole(FR, 2, 2 * COLS, C),
        scratch_shapes=[
            pltpu.VMEM((576, 2 * C), bf),
            pltpu.VMEM((4, 4, 2 * COLS + TOK, C), bf),
            pltpu.VMEM((4 * TOK, C), jnp.float32),
            pltpu.VMEM((FR, 2, 3, 2 * COLS, 128), jnp.float32),
        ],
        compiler_params=pltpu.CompilerParams(vmem_limit_bytes=32 << 20),
        name="decode",
    )(
        cells,
        conv_in_weight.reshape(9, 3 * LAT, C),
        vecs,
        conv_weight.reshape(9, 3 * C, C),
    )


def solution(mesh):
    cut = P("video", "row", None, None)
    part = P("video")
    return jax.shard_map(
        functools.partial(shards, mesh.shape["row"]),
        mesh=mesh,
        in_specs=(cut,) * 4 + (part,) * 3 + (P(),) * 9,
        out_specs=cut,
        check_vma=False,
    )
```

```python
import functools

import jax
import jax.numpy as jnp
from jax import lax
from jax.experimental import pallas as pl
from jax.experimental.pallas import tpu as pltpu
from jax.sharding import PartitionSpec as P

HEADS = 12
LAT = 16
GROUP = 4
HPD = HEADS // GROUP
HD = 128
FR = 4
COLS = 32
TOK = FR * COLS
ROWS_EXT = GROUP + 6
KEYS = FR * 7 * COLS
C = 384
NEG = -1e30
LIMIT = 62 << 20


def lanes(ref):
    return jnp.concatenate([ref[i : i + 1] for i in range(ref.shape[0])], axis=-1)


def attend_kernel(
    n_rows,
    stream_hbm,
    q_ref,
    k_ref,
    v_ref,
    gate_hbm,
    shift_hbm,
    scale_hbm,
    hw_hbm,
    hb_hbm,
    mean_hbm,
    std_hbm,
    cw_hbm,
    cib_hbm,
    gain_hbm,
    cb_hbm,
    w_hbm,
    out_hbm,
    w4_ref,
    w_ref,
    cib_ref,
    gain_ref,
    cb_ref,
    stream_ref,
    gate_ref,
    shift_ref,
    scale_ref,
    hw_ref,
    hb_ref,
    mean_ref,
    std_ref,
    cw_ref,
    load_sem,
    qb,
    kb,
    vb,
    ob,
    attn,
    bias,
    gbuf,
    own_sem,
    s1,
    r1,
    s2,
    r2,
    s3,
    r3,
    s4,
    r4,
    var,
    acc,
    wide,
    done,
    out_sem,
):
    row = lax.axis_index("row")
    g = row // GROUP
    j = row % GROUP
    groups = n_rows // GROUP
    has_up = g > 0
    has_down = g < groups - 1
    first = row == 0
    last = row == n_rows - 1

    def head_cols(p, h):
        return pl.ds(pl.multiple_of((p * HPD + h) * HD, HD), HD)

    srcs = (k_ref, v_ref, q_ref)

    def level_dst(x, h, idx):
        if x == 2:
            return qb.at[h, idx]
        return (kb, vb)[x].at[h, :, idx + 3]

    own = []
    for h in range(HPD):
        for x in range(3):
            cp = pltpu.make_async_copy(
                srcs[x].at[:, :, head_cols(j, h)], level_dst(x, h, j), own_sem.at[x, h]
            )
            cp.start()
            own.append(cp)

    barrier = pltpu.get_barrier_semaphore()
    for d in range(1, GROUP):
        pl.semaphore_signal(barrier, inc=1, device_id={"row": g * GROUP + (j + d) % GROUP})

    @pl.when(has_up)
    def _():
        pl.semaphore_signal(barrier, inc=1, device_id={"row": row - GROUP})

    @pl.when(has_down)
    def _():
        pl.semaphore_signal(barrier, inc=1, device_id={"row": row + GROUP})

    cross_up = jnp.logical_and(j == 0, has_up)
    cross_down = jnp.logical_and(j == GROUP - 1, has_down)

    @pl.when(cross_up)
    def _():
        pl.semaphore_signal(barrier, inc=1, device_id={"row": row - 1})

    @pl.when(cross_down)
    def _():
        pl.semaphore_signal(barrier, inc=1, device_id={"row": row + 1})

    one = jnp.int32(1)
    zero = jnp.int32(0)
    expected = (
        3
        + jnp.where(has_up, one, zero)
        + jnp.where(has_down, one, zero)
        + jnp.where(cross_up, one, zero)
        + jnp.where(cross_down, one, zero)
    )
    pl.semaphore_wait(barrier, expected)

    def level_copy(x, h, d):
        p = (j + d) % GROUP
        return pltpu.make_async_remote_copy(
            src_ref=srcs[x].at[:, :, head_cols(p, h)],
            dst_ref=level_dst(x, h, j),
            send_sem=s1.at[x, h, d - 1],
            recv_sem=r1.at[x, h, d - 1],
            device_id={"row": g * GROUP + p},
        )

    for h in range(HPD):
        for x in range(2):
            for d in (2, 1, 3):
                level_copy(x, h, d).start()
    for h in range(HPD):
        for d in (2, 1, 3):
            level_copy(2, h, d).start()

    def edge_copy(x, h, up):
        buf = (kb, vb)[x]
        if up:
            src, dst, dev = buf.at[h, :, pl.ds(3, 3)], buf.at[h, :, pl.ds(7, 3)], row - GROUP
        else:
            src, dst, dev = buf.at[h, :, pl.ds(4, 3)], buf.at[h, :, pl.ds(0, 3)], row + GROUP
        way = 0 if up else 1
        return pltpu.make_async_remote_copy(
            src_ref=src,
            dst_ref=dst,
            send_sem=s2.at[x, h, way],
            recv_sem=r2.at[x, h, way],
            device_id={"row": dev},
        )

    pairs = (
        (stream_hbm, stream_ref),
        (gate_hbm, gate_ref),
        (shift_hbm, shift_ref),
        (scale_hbm, scale_ref),
        (hw_hbm, hw_ref),
        (hb_hbm, hb_ref),
        (mean_hbm, mean_ref),
        (std_hbm, std_ref),
        (cw_hbm, cw_ref),
        (cib_hbm, cib_ref),
        (gain_hbm, gain_ref),
        (cb_hbm, cb_ref),
        (w_hbm, w_ref),
    )
    loads = [
        pltpu.make_async_copy(src, dst, load_sem.at[i]) for i, (src, dst) in enumerate(pairs)
    ]
    for cp in loads:
        cp.start()

    tok_i = lax.broadcasted_iota(jnp.int32, (TOK, KEYS), 0)
    key_i = lax.broadcasted_iota(jnp.int32, (TOK, KEYS), 1)
    t = tok_i >> 5
    w = tok_i & 31
    span = 7 * COLS
    f = (
        jnp.where(key_i >= span, 1, 0)
        + jnp.where(key_i >= 2 * span, 1, 0)
        + jnp.where(key_i >= 3 * span, 1, 0)
    )
    fs = jnp.clip(t - 1, 0, FR - 3)
    cs = jnp.clip(w - 3, 0, COLS - 7)
    vcol = key_i & 31
    ok = (f >= fs) & (f < fs + 3) & (vcol >= cs) & (vcol < cs + 7)
    bias[...] = jnp.where(ok, 0.0, NEG)

    empty = jnp.zeros((HPD, FR, 3, COLS, HD), jnp.bfloat16)

    @pl.when(jnp.logical_not(has_up))
    def _():
        kb[:, :, 0:3] = empty
        vb[:, :, 0:3] = empty

    @pl.when(jnp.logical_not(has_down))
    def _():
        kb[:, :, 7:10] = empty
        vb[:, :, 7:10] = empty

    @pl.when(first)
    def _():
        gbuf[0] = jnp.zeros((TOK, 128), jnp.bfloat16)

    @pl.when(last)
    def _():
        gbuf[2] = jnp.zeros((TOK, 128), jnp.bfloat16)

    for cp in own:
        cp.wait()
    for cp in loads[:-1]:
        cp.wait()

    w4_ref[...] = jnp.zeros(w4_ref.shape, jnp.bfloat16)
    for ab in range(9):
        w4_ref[ab * 64 : ab * 64 + 48, 0:C] = cw_ref[ab]
        w4_ref[ab * 64 + 16 : ab * 64 + 64, C : 2 * C] = cw_ref[ab]

    for h in range(HPD):
        for x in range(2):
            for d in range(1, GROUP):
                level_copy(x, h, d).wait_recv()

            @pl.when(has_up)
            def _():
                edge_copy(x, h, True).start()

            @pl.when(has_down)
            def _():
                edge_copy(x, h, False).start()

    key_row = lax.broadcasted_iota(jnp.int32, (1, KEYS), 1)
    fr = (
        jnp.where(key_row >= span, 1, 0)
        + jnp.where(key_row >= 2 * span, 1, 0)
        + jnp.where(key_row >= 3 * span, 1, 0)
    )
    rel_row = (key_row >> 5) - 7 * fr + (GROUP * g - 3)

    def out_copy(h, d):
        p = (j + d) % GROUP
        return pltpu.make_async_remote_copy(
            src_ref=ob.at[h, p],
            dst_ref=attn.at[j * HPD + h],
            send_sem=s3.at[h, d - 1],
            recv_sem=r3.at[h, d - 1],
            device_id={"row": g * GROUP + p},
        )

    for h in range(HPD):
        for d in range(1, GROUP):
            level_copy(2, h, d).wait_recv()
        for x in range(2):

            @pl.when(has_down)
            def _():
                edge_copy(x, h, True).wait_recv()

            @pl.when(has_up)
            def _():
                edge_copy(x, h, False).wait_recv()

        def one_row(i, carry):
            qm = qb[h, i].reshape(TOK, HD)
            km = kb[h, :, pl.ds(i, 7)].reshape(KEYS, HD)
            vm = vb[h, :, pl.ds(i, 7)].reshape(KEYS, HD)
            s = lax.dot_general(
                qm, km, (((1,), (1,)), ((), ())), preferred_element_type=jnp.float32
            )
            src_row = rel_row + i
            row_bias = jnp.where((src_row >= 0) & (src_row < n_rows), 0.0, NEG)
            s = s * (HD**-0.5) + (bias[...] + row_bias)
            m = jnp.max(s, axis=1, keepdims=True)
            e = jnp.exp(s - m)
            l = jnp.sum(e, axis=1, keepdims=True)
            pr = (e * (1.0 / l)).astype(jnp.bfloat16)
            o = jnp.dot(pr, vm, preferred_element_type=jnp.float32)
            ob[h, i] = o.astype(jnp.bfloat16)
            return carry

        lax.fori_loop(0, GROUP, one_row, 0)
        for d in (2, 1, 3):
            out_copy(h, d).start()
        attn[j * HPD + h] = ob[h, j]

    for h in range(HPD):
        for d in range(1, GROUP):
            out_copy(h, d).wait_recv()

    attn_all = jnp.concatenate([attn[c] for c in range(HEADS)], axis=-1)
    resid = stream_ref[...].astype(jnp.float32) + lanes(gate_ref) * attn_all.astype(jnp.float32)
    center = resid - jnp.mean(resid, axis=-1, keepdims=True)
    spread = jnp.mean(center * center, axis=-1, keepdims=True)
    normed = center * lax.rsqrt(spread + 1e-06) * (1.0 + lanes(scale_ref)) + lanes(shift_ref)
    patch = lax.dot_general(
        normed.astype(jnp.bfloat16),
        hw_ref[...],
        (((1,), (1,)), ((), ())),
        preferred_element_type=jnp.float32,
    )
    patch = patch + hb_ref[...]
    std = jnp.concatenate([std_ref[...]] * 4, axis=-1)
    mean = jnp.concatenate([mean_ref[...]] * 4, axis=-1)
    latent = (patch * std + mean).astype(jnp.bfloat16)

    dst_l = lax.broadcasted_iota(jnp.int32, (4 * LAT, 128), 1)
    src_l = lax.broadcasted_iota(jnp.int32, (4 * LAT, 128), 0)
    part = (dst_l >> 4) & 3
    want = ((dst_l >> 6) * 2 + (1 - (part & 1))) * LAT + (dst_l & 15)
    pick = jnp.where(src_l == want, 1.0, 0.0).astype(jnp.bfloat16)
    spreadout = jnp.dot(latent, pick, preferred_element_type=jnp.float32)
    lane = lax.broadcasted_iota(jnp.int32, (TOK, 128), 1)
    col = lax.broadcasted_iota(jnp.int32, (TOK, 128), 0) & 31
    lane_part = (lane >> 4) & 3
    before = jnp.where(col == 0, 0.0, pltpu.roll(spreadout, 1, 0))
    after = jnp.where(col == COLS - 1, 0.0, pltpu.roll(spreadout, TOK - 1, 0))
    cells = jnp.where(lane_part == 0, before, jnp.where(lane_part == 3, after, spreadout))
    gbuf[1] = cells.astype(jnp.bfloat16)

    def latent_copy(up):
        way = 0 if up else 1
        return pltpu.make_async_remote_copy(
            src_ref=gbuf.at[1],
            dst_ref=gbuf.at[2 if up else 0],
            send_sem=s4.at[way],
            recv_sem=r4.at[way],
            device_id={"row": row - 1 if up else row + 1},
        )

    @pl.when(jnp.logical_not(first))
    def _():
        latent_copy(True).start()

    @pl.when(jnp.logical_not(last))
    def _():
        latent_copy(False).start()

    for h in range(HPD):
        for x in range(3):
            for d in range(1, GROUP):
                level_copy(x, h, d).wait_send()
        for x in range(2):

            @pl.when(has_up)
            def _():
                edge_copy(x, h, True).wait_send()

            @pl.when(has_down)
            def _():
                edge_copy(x, h, False).wait_send()

        for d in range(1, GROUP):
            out_copy(h, d).wait_send()

    @pl.when(jnp.logical_not(first))
    def _():
        latent_copy(True).wait_send()
        latent_copy(False).wait_recv()

    @pl.when(jnp.logical_not(last))
    def _():
        latent_copy(False).wait_send()
        latent_copy(True).wait_recv()

    loads[-1].wait()
    decode(
        row, n_rows, gbuf, w4_ref, w_ref, cib_ref, gain_ref, cb_ref, out_hbm, var, acc, wide, done,
        out_sem,
    )


def decode(
    row, n_rows, cells_ref, w4_ref, w_ref, cib_ref, gain_ref, cb_ref, out_hbm, var, acc, wide, done,
    sem,
):
    six = jnp.concatenate([cells_ref[i] for i in range(3)], axis=-1)
    col = lax.broadcasted_iota(jnp.int32, (TOK, C), 0) & 31
    zeros = jnp.zeros((2 * COLS, C), jnp.bfloat16)
    pad = jnp.zeros((2 * COLS, 192), jnp.bfloat16)
    for y in range(4):
        rows3 = six[:, y * 64 : y * 64 + 192]
        padded = jnp.concatenate([pad, rows3], axis=0)
        x = jnp.concatenate([padded[i * COLS : i * COLS + TOK] for i in range(3)], axis=-1)
        h = jnp.dot(x, w4_ref[...], preferred_element_type=jnp.float32)
        acts = []
        for q in range(2):
            hidden = (h[:, q * C : (q + 1) * C] + lanes(cib_ref)).astype(jnp.bfloat16)
            hidden = hidden.astype(jnp.float32)
            if y in (1, 2):
                at = ((y - 1) * 2 + q) * TOK
                acc[at : at + TOK, :] = hidden + lanes(cb_ref)
            ms = jnp.mean(hidden * hidden, axis=-1, keepdims=True)
            scaled = hidden * lax.rsqrt(ms + 1e-06) * lanes(gain_ref)
            act = scaled / (1.0 + jnp.exp(-scaled))
            if y == 0:
                act = jnp.where(row > 0, act, 0.0)
            if y == 3:
                act = jnp.where(row < n_rows - 1, act, 0.0)
            acts.append(act)
        before = jnp.where(col == 0, 0.0, pltpu.roll(acts[1], 1, 0))
        after = jnp.where(col == COLS - 1, 0.0, pltpu.roll(acts[0], TOK - 1, 0))
        for i, piece in enumerate((before, acts[0], acts[1], after)):
            var[i, y, 0 : 2 * COLS] = zeros
            var[i, y, 2 * COLS :] = piece.astype(jnp.bfloat16)

    for a in range(3):
        for b in range(3):
            phases = []
            for y in range(2):
                taps = [var[i, y + b, a * COLS : a * COLS + TOK] for i in range(4)]
                for q in range(2):
                    phases.append(jnp.concatenate(taps[q : q + 3], axis=-1))
            lhs = jnp.concatenate(phases, axis=0)
            acc[...] += jnp.dot(lhs, w_ref[a * 3 + b], preferred_element_type=jnp.float32)

    copies = []
    for t in range(FR):
        for y in range(2):
            for q in range(2):
                at = (y * 2 + q) * TOK + t * COLS
                for c in range(3):
                    wide[t, y, c, pl.ds(q, COLS, stride=2), :] = acc[
                        at : at + COLS, c * 128 : (c + 1) * 128
                    ]
        for c in range(3):
            done[t, :, :, c * 128 : (c + 1) * 128] = wide[t, :, c].astype(jnp.bfloat16)
        cp = pltpu.make_async_copy(done.at[t], out_hbm.at[t], sem.at[t])
        cp.start()
        copies.append(cp)
    for cp in copies:
        cp.wait()


def shards(
    n_rows,
    stream,
    query,
    key,
    value,
    attn_gate,
    shift_mod,
    scale_mod,
    head_weight,
    head_bias,
    latent_mean,
    latent_std,
    conv_in_weight,
    conv_in_bias,
    norm_gain,
    conv_weight,
    conv_bias,
):
    width = query.shape[-1]
    flat = (FR, COLS, width)
    hbm = pl.BlockSpec(memory_space=pltpu.HBM)
    dma = pltpu.SemaphoreType.DMA
    bf = jnp.bfloat16
    f32 = jnp.float32
    line = lambda x: x.reshape(-1, min(128, x.shape[0]))
    shape = jax.ShapeDtypeStruct
    return pl.pallas_call(
        functools.partial(attend_kernel, n_rows),
        out_shape=shape((FR, 2, 2 * COLS, C), bf),
        in_specs=[hbm] * 16,
        out_specs=hbm,
        scratch_shapes=[
            pltpu.VMEM((576, 2 * C), bf),
            pltpu.VMEM((9, 3 * C, C), bf),
            pltpu.VMEM((C // 128, 128), f32),
            pltpu.VMEM((C // 128, 128), f32),
            pltpu.VMEM((C // 128, 128), f32),
            pltpu.VMEM((TOK, width), bf),
            pltpu.VMEM((width // 128, 128), f32),
            pltpu.VMEM((width // 128, 128), f32),
            pltpu.VMEM((width // 128, 128), f32),
            pltpu.VMEM((4 * LAT, width), bf),
            pltpu.VMEM((1, 4 * LAT), f32),
            pltpu.VMEM((1, LAT), f32),
            pltpu.VMEM((1, LAT), f32),
            pltpu.VMEM((9, 3 * LAT, C), bf),
            dma((13,)),
            pltpu.VMEM((HPD, GROUP, FR, COLS, HD), bf),
            pltpu.VMEM((HPD, FR, ROWS_EXT, COLS, HD), bf),
            pltpu.VMEM((HPD, FR, ROWS_EXT, COLS, HD), bf),
            pltpu.VMEM((HPD, GROUP, TOK, HD), bf),
            pltpu.VMEM((HEADS, TOK, HD), bf),
            pltpu.VMEM((TOK, KEYS), f32),
            pltpu.VMEM((3, TOK, 128), bf),
            dma((3, HPD)),
            dma((3, HPD, 3)),
            dma((3, HPD, 3)),
            dma((2, HPD, 2)),
            dma((2, HPD, 2)),
            dma((HPD, 3)),
            dma((HPD, 3)),
            dma((2,)),
            dma((2,)),
            pltpu.VMEM((4, 4, 2 * COLS + TOK, C), bf),
            pltpu.VMEM((4 * TOK, C), f32),
            pltpu.VMEM((FR, 2, 3, 2 * COLS, 128), f32),
            pltpu.VMEM((FR, 2, 2 * COLS, C), bf),
            dma((FR,)),
        ],
        compiler_params=pltpu.CompilerParams(
            collective_id=0, has_side_effects=True, vmem_limit_bytes=LIMIT
        ),
        name="attend",
    )(
        stream.reshape(TOK, width),
        query.reshape(flat),
        key.reshape(flat),
        value.reshape(flat),
        line(attn_gate),
        line(shift_mod),
        line(scale_mod),
        head_weight.T,
        line(head_bias),
        line(latent_mean),
        line(latent_std),
        conv_in_weight.reshape(9, 3 * LAT, C),
        line(conv_in_bias),
        line(norm_gain),
        line(conv_bias),
        conv_weight.reshape(9, 3 * C, C),
    )


def solution(mesh):
    cut = P("video", "row", None, None)
    part = P("video")
    return jax.shard_map(
        functools.partial(shards, mesh.shape["row"]),
        mesh=mesh,
        in_specs=(cut,) * 4 + (part,) * 3 + (P(),) * 9,
        out_specs=cut,
        check_vma=False,
    )
```

```python
import functools

import jax
import jax.numpy as jnp
from jax import lax
from jax.experimental import pallas as pl
from jax.experimental.pallas import tpu as pltpu
from jax.sharding import PartitionSpec as P

HEADS = 12
LAT = 16
GROUP = 4
HPD = HEADS // GROUP
HD = 128
FR = 4
COLS = 32
TOK = FR * COLS
ROWS_EXT = GROUP + 6
KEYS = FR * 7 * COLS
C = 384
NEG = -1e30
LIMIT = 62 << 20


def lanes(ref):
    return jnp.concatenate([ref[i : i + 1] for i in range(ref.shape[0])], axis=-1)


def attend_kernel(
    n_rows,
    stream_hbm,
    q_ref,
    k_ref,
    v_ref,
    gate_hbm,
    shift_hbm,
    scale_hbm,
    hw_hbm,
    hb_hbm,
    mean_hbm,
    std_hbm,
    cw_hbm,
    cib_hbm,
    gain_hbm,
    cb_hbm,
    w_hbm,
    out_hbm,
    w4_ref,
    w_ref,
    cib_ref,
    gain_ref,
    cb_ref,
    stream_ref,
    gate_ref,
    shift_ref,
    scale_ref,
    hw_ref,
    hb_ref,
    mean_ref,
    std_ref,
    cw_ref,
    load_sem,
    qb,
    kb,
    vb,
    ob,
    attn,
    bias,
    gbuf,
    own_sem,
    s1,
    r1,
    s2,
    r2,
    s5,
    r5,
    s3,
    r3,
    s4,
    r4,
    var,
    acc,
    wide,
    done,
    out_sem,
):
    row = lax.axis_index("row")
    g = row // GROUP
    j = row % GROUP
    groups = n_rows // GROUP
    half = j // 2
    mate = j + 1 - 2 * (j % 2)
    has_up = g > 0
    has_down = g < groups - 1
    first = row == 0
    last = row == n_rows - 1

    def head_cols(p, h):
        return pl.ds(pl.multiple_of((p * HPD + h) * HD, HD), HD)

    srcs = (k_ref, v_ref, q_ref)

    def level_dst(x, h, idx):
        if x == 2:
            return qb.at[h, idx]
        return (kb, vb)[x].at[h, :, idx + 3]

    own = []
    for h in range(HPD):
        for x in range(3):
            cp = pltpu.make_async_copy(
                srcs[x].at[:, :, head_cols(j, h)], level_dst(x, h, j), own_sem.at[x, h]
            )
            cp.start()
            own.append(cp)

    barrier = pltpu.get_barrier_semaphore()
    for d in range(1, GROUP):
        pl.semaphore_signal(barrier, inc=1, device_id={"row": g * GROUP + (j + d) % GROUP})

    @pl.when(has_up)
    def _():
        for p in (j, mate):
            pl.semaphore_signal(barrier, inc=1, device_id={"row": (g - 1) * GROUP + p})

    @pl.when(has_down)
    def _():
        for p in (j, mate):
            pl.semaphore_signal(barrier, inc=1, device_id={"row": (g + 1) * GROUP + p})

    cross_up = jnp.logical_and(j == 0, has_up)
    cross_down = jnp.logical_and(j == GROUP - 1, has_down)

    @pl.when(cross_up)
    def _():
        pl.semaphore_signal(barrier, inc=1, device_id={"row": row - 1})

    @pl.when(cross_down)
    def _():
        pl.semaphore_signal(barrier, inc=1, device_id={"row": row + 1})

    one = jnp.int32(1)
    zero = jnp.int32(0)
    expected = (
        3
        + 2 * jnp.where(has_up, one, zero)
        + 2 * jnp.where(has_down, one, zero)
        + jnp.where(cross_up, one, zero)
        + jnp.where(cross_down, one, zero)
    )
    pl.semaphore_wait(barrier, expected)

    def level_copy(x, h, d):
        p = (j + d) % GROUP
        return pltpu.make_async_remote_copy(
            src_ref=srcs[x].at[:, :, head_cols(p, h)],
            dst_ref=level_dst(x, h, j),
            send_sem=s1.at[x, h, d - 1],
            recv_sem=r1.at[x, h, d - 1],
            device_id={"row": g * GROUP + p},
        )

    def relay_copy(x, h, two):
        buf = (kb, vb)[x]
        if two:
            src, dst = buf.at[h, :, pl.ds(5 - 2 * half, 2)], buf.at[h, :, pl.ds(1 + 6 * half, 2)]
            dev = row + GROUP - 2 * GROUP * half
        else:
            src, dst = buf.at[h, :, pl.ds(5 - half, 1)], buf.at[h, :, pl.ds(9 - 9 * half, 1)]
            dev = row - GROUP + 2 * GROUP * half
        way = 0 if two else 1
        return pltpu.make_async_remote_copy(
            src_ref=src,
            dst_ref=dst,
            send_sem=s2.at[x, h, way],
            recv_sem=r2.at[x, h, way],
            device_id={"row": dev},
        )

    ahead = jnp.logical_or(
        jnp.logical_and(half == 0, has_down), jnp.logical_and(half == 1, has_up)
    )
    behind = jnp.logical_or(
        jnp.logical_and(half == 0, has_up), jnp.logical_and(half == 1, has_down)
    )

    def straight_copy(x, h, up, c, at):
        p = (j, mate)[c]
        way = 0 if up else 1
        return pltpu.make_async_remote_copy(
            src_ref=srcs[x].at[:, :, head_cols(p, h)],
            dst_ref=(kb, vb)[x].at[h, :, at],
            send_sem=s5.at[x, h, way, c],
            recv_sem=r5.at[x, h, way, c],
            device_id={"row": (g - 1 if up else g + 1) * GROUP + p},
        )

    send_up = jnp.logical_and(has_up, j <= 2)
    send_down = jnp.logical_and(has_down, j >= 1)
    recv_up = [jnp.logical_and(has_down, p <= 2) for p in (j, mate)]
    recv_down = [jnp.logical_and(has_up, p >= 1) for p in (j, mate)]

    for h in range(HPD):
        for x in range(2):
            for d in (2, 1, 3):
                level_copy(x, h, d).start()

        @pl.when(send_up)
        def _():
            for x in range(2):
                for c in range(2):
                    straight_copy(x, h, True, c, 7 + j).start()

        @pl.when(send_down)
        def _():
            for x in range(2):
                for c in range(2):
                    straight_copy(x, h, False, c, j - 1).start()

    for h in range(HPD):
        for d in (2, 1, 3):
            level_copy(2, h, d).start()

    pairs = (
        (stream_hbm, stream_ref),
        (gate_hbm, gate_ref),
        (shift_hbm, shift_ref),
        (scale_hbm, scale_ref),
        (hw_hbm, hw_ref),
        (hb_hbm, hb_ref),
        (mean_hbm, mean_ref),
        (std_hbm, std_ref),
        (cw_hbm, cw_ref),
        (cib_hbm, cib_ref),
        (gain_hbm, gain_ref),
        (cb_hbm, cb_ref),
        (w_hbm, w_ref),
    )
    loads = [
        pltpu.make_async_copy(src, dst, load_sem.at[i]) for i, (src, dst) in enumerate(pairs)
    ]
    for cp in loads:
        cp.start()

    tok_i = lax.broadcasted_iota(jnp.int32, (TOK, KEYS), 0)
    key_i = lax.broadcasted_iota(jnp.int32, (TOK, KEYS), 1)
    t = tok_i >> 5
    w = tok_i & 31
    span = 7 * COLS
    f = (
        jnp.where(key_i >= span, 1, 0)
        + jnp.where(key_i >= 2 * span, 1, 0)
        + jnp.where(key_i >= 3 * span, 1, 0)
    )
    fs = jnp.clip(t - 1, 0, FR - 3)
    cs = jnp.clip(w - 3, 0, COLS - 7)
    vcol = key_i & 31
    ok = (f >= fs) & (f < fs + 3) & (vcol >= cs) & (vcol < cs + 7)
    bias[...] = jnp.where(ok, 0.0, NEG)

    empty = jnp.zeros((HPD, FR, 3, COLS, HD), jnp.bfloat16)

    @pl.when(jnp.logical_not(has_up))
    def _():
        kb[:, :, 0:3] = empty
        vb[:, :, 0:3] = empty

    @pl.when(jnp.logical_not(has_down))
    def _():
        kb[:, :, 7:10] = empty
        vb[:, :, 7:10] = empty

    @pl.when(first)
    def _():
        gbuf[0] = jnp.zeros((TOK, 128), jnp.bfloat16)

    @pl.when(last)
    def _():
        gbuf[2] = jnp.zeros((TOK, 128), jnp.bfloat16)

    for cp in own:
        cp.wait()
    for cp in loads[:-1]:
        cp.wait()

    w4_ref[...] = jnp.zeros(w4_ref.shape, jnp.bfloat16)
    for ab in range(9):
        w4_ref[ab * 64 : ab * 64 + 48, 0:C] = cw_ref[ab]
        w4_ref[ab * 64 + 16 : ab * 64 + 64, C : 2 * C] = cw_ref[ab]

    for h in range(HPD):
        for x in range(2):
            for d in range(1, GROUP):
                level_copy(x, h, d).wait_recv()

            @pl.when(ahead)
            def _():
                relay_copy(x, h, True).start()

            @pl.when(behind)
            def _():
                relay_copy(x, h, False).start()

    key_row = lax.broadcasted_iota(jnp.int32, (1, KEYS), 1)
    fr = (
        jnp.where(key_row >= span, 1, 0)
        + jnp.where(key_row >= 2 * span, 1, 0)
        + jnp.where(key_row >= 3 * span, 1, 0)
    )
    rel_row = (key_row >> 5) - 7 * fr + (GROUP * g - 3)

    def out_copy(h, d):
        p = (j + d) % GROUP
        return pltpu.make_async_remote_copy(
            src_ref=ob.at[h, p],
            dst_ref=attn.at[j * HPD + h],
            send_sem=s3.at[h, d - 1],
            recv_sem=r3.at[h, d - 1],
            device_id={"row": g * GROUP + p},
        )

    for h in range(HPD):
        for d in range(1, GROUP):
            level_copy(2, h, d).wait_recv()
        for x in range(2):

            @pl.when(behind)
            def _():
                relay_copy(x, h, True).wait_recv()

            @pl.when(ahead)
            def _():
                relay_copy(x, h, False).wait_recv()

            for c in range(2):

                @pl.when(recv_up[c])
                def _():
                    straight_copy(x, h, True, c, 7).wait_recv()

                @pl.when(recv_down[c])
                def _():
                    straight_copy(x, h, False, c, 0).wait_recv()

        def one_row(i):
            qm = qb[h, i].reshape(TOK, HD)
            km = kb[h, :, pl.ds(i, 7)].reshape(KEYS, HD)
            vm = vb[h, :, pl.ds(i, 7)].reshape(KEYS, HD)
            s = lax.dot_general(
                qm, km, (((1,), (1,)), ((), ())), preferred_element_type=jnp.float32
            )
            src_row = rel_row + i
            row_bias = jnp.where((src_row >= 0) & (src_row < n_rows), 0.0, NEG)
            s = s * (HD**-0.5) + (bias[...] + row_bias)
            m = jnp.max(s, axis=1, keepdims=True)
            e = jnp.exp(s - m)
            l = jnp.sum(e, axis=1, keepdims=True)
            pr = (e * (1.0 / l)).astype(jnp.bfloat16)
            o = jnp.dot(pr, vm, preferred_element_type=jnp.float32)
            return o.astype(jnp.bfloat16)

        for d in (2, 1, 3):
            i = (j + d) % GROUP
            ob[h, i] = one_row(i)
            out_copy(h, d).start()
        attn[j * HPD + h] = one_row(j)

    for h in range(HPD):
        for d in range(1, GROUP):
            out_copy(h, d).wait_recv()

    attn_all = jnp.concatenate([attn[c] for c in range(HEADS)], axis=-1)
    resid = stream_ref[...].astype(jnp.float32) + lanes(gate_ref) * attn_all.astype(jnp.float32)
    center = resid - jnp.mean(resid, axis=-1, keepdims=True)
    spread = jnp.mean(center * center, axis=-1, keepdims=True)
    normed = center * lax.rsqrt(spread + 1e-06) * (1.0 + lanes(scale_ref)) + lanes(shift_ref)
    patch = lax.dot_general(
        normed.astype(jnp.bfloat16),
        hw_ref[...],
        (((1,), (1,)), ((), ())),
        preferred_element_type=jnp.float32,
    )
    patch = patch + hb_ref[...]
    std = jnp.concatenate([std_ref[...]] * 4, axis=-1)
    mean = jnp.concatenate([mean_ref[...]] * 4, axis=-1)
    latent = (patch * std + mean).astype(jnp.bfloat16)

    dst_l = lax.broadcasted_iota(jnp.int32, (4 * LAT, 128), 1)
    src_l = lax.broadcasted_iota(jnp.int32, (4 * LAT, 128), 0)
    part = (dst_l >> 4) & 3
    want = ((dst_l >> 6) * 2 + (1 - (part & 1))) * LAT + (dst_l & 15)
    pick = jnp.where(src_l == want, 1.0, 0.0).astype(jnp.bfloat16)
    spreadout = jnp.dot(latent, pick, preferred_element_type=jnp.float32)
    lane = lax.broadcasted_iota(jnp.int32, (TOK, 128), 1)
    col = lax.broadcasted_iota(jnp.int32, (TOK, 128), 0) & 31
    lane_part = (lane >> 4) & 3
    before = jnp.where(col == 0, 0.0, pltpu.roll(spreadout, 1, 0))
    after = jnp.where(col == COLS - 1, 0.0, pltpu.roll(spreadout, TOK - 1, 0))
    cells = jnp.where(lane_part == 0, before, jnp.where(lane_part == 3, after, spreadout))
    gbuf[1] = cells.astype(jnp.bfloat16)

    def latent_copy(up):
        way = 0 if up else 1
        return pltpu.make_async_remote_copy(
            src_ref=gbuf.at[1],
            dst_ref=gbuf.at[2 if up else 0],
            send_sem=s4.at[way],
            recv_sem=r4.at[way],
            device_id={"row": row - 1 if up else row + 1},
        )

    @pl.when(jnp.logical_not(first))
    def _():
        latent_copy(True).start()

    @pl.when(jnp.logical_not(last))
    def _():
        latent_copy(False).start()

    for h in range(HPD):
        for x in range(3):
            for d in range(1, GROUP):
                level_copy(x, h, d).wait_send()
        for x in range(2):

            @pl.when(ahead)
            def _():
                relay_copy(x, h, True).wait_send()

            @pl.when(behind)
            def _():
                relay_copy(x, h, False).wait_send()

            @pl.when(send_up)
            def _():
                for c in range(2):
                    straight_copy(x, h, True, c, 7).wait_send()

            @pl.when(send_down)
            def _():
                for c in range(2):
                    straight_copy(x, h, False, c, 0).wait_send()

        for d in range(1, GROUP):
            out_copy(h, d).wait_send()

    @pl.when(jnp.logical_not(first))
    def _():
        latent_copy(True).wait_send()
        latent_copy(False).wait_recv()

    @pl.when(jnp.logical_not(last))
    def _():
        latent_copy(False).wait_send()
        latent_copy(True).wait_recv()

    loads[-1].wait()
    decode(
        row, n_rows, gbuf, w4_ref, w_ref, cib_ref, gain_ref, cb_ref, out_hbm, var, acc, wide, done,
        out_sem,
    )


def decode(
    row, n_rows, cells_ref, w4_ref, w_ref, cib_ref, gain_ref, cb_ref, out_hbm, var, acc, wide, done,
    sem,
):
    six = jnp.concatenate([cells_ref[i] for i in range(3)], axis=-1)
    col = lax.broadcasted_iota(jnp.int32, (TOK, C), 0) & 31
    zeros = jnp.zeros((2 * COLS, C), jnp.bfloat16)
    pad = jnp.zeros((2 * COLS, 192), jnp.bfloat16)
    for y in range(4):
        rows3 = six[:, y * 64 : y * 64 + 192]
        padded = jnp.concatenate([pad, rows3], axis=0)
        x = jnp.concatenate([padded[i * COLS : i * COLS + TOK] for i in range(3)], axis=-1)
        h = jnp.dot(x, w4_ref[...], preferred_element_type=jnp.float32)
        acts = []
        for q in range(2):
            hidden = (h[:, q * C : (q + 1) * C] + lanes(cib_ref)).astype(jnp.bfloat16)
            hidden = hidden.astype(jnp.float32)
            if y in (1, 2):
                at = ((y - 1) * 2 + q) * TOK
                acc[at : at + TOK, :] = hidden + lanes(cb_ref)
            ms = jnp.mean(hidden * hidden, axis=-1, keepdims=True)
            scaled = hidden * lax.rsqrt(ms + 1e-06) * lanes(gain_ref)
            act = scaled / (1.0 + jnp.exp(-scaled))
            if y == 0:
                act = jnp.where(row > 0, act, 0.0)
            if y == 3:
                act = jnp.where(row < n_rows - 1, act, 0.0)
            acts.append(act)
        before = jnp.where(col == 0, 0.0, pltpu.roll(acts[1], 1, 0))
        after = jnp.where(col == COLS - 1, 0.0, pltpu.roll(acts[0], TOK - 1, 0))
        for i, piece in enumerate((before, acts[0], acts[1], after)):
            var[i, y, 0 : 2 * COLS] = zeros
            var[i, y, 2 * COLS :] = piece.astype(jnp.bfloat16)

    for a in range(3):
        for b in range(3):
            phases = []
            for y in range(2):
                taps = [var[i, y + b, a * COLS : a * COLS + TOK] for i in range(4)]
                for q in range(2):
                    phases.append(jnp.concatenate(taps[q : q + 3], axis=-1))
            lhs = jnp.concatenate(phases, axis=0)
            acc[...] += jnp.dot(lhs, w_ref[a * 3 + b], preferred_element_type=jnp.float32)

    copies = []
    for t in range(FR):
        for y in range(2):
            for q in range(2):
                at = (y * 2 + q) * TOK + t * COLS
                for c in range(3):
                    wide[t, y, c, pl.ds(q, COLS, stride=2), :] = acc[
                        at : at + COLS, c * 128 : (c + 1) * 128
                    ]
        for c in range(3):
            done[t, :, :, c * 128 : (c + 1) * 128] = wide[t, :, c].astype(jnp.bfloat16)
        cp = pltpu.make_async_copy(done.at[t], out_hbm.at[t], sem.at[t])
        cp.start()
        copies.append(cp)
    for cp in copies:
        cp.wait()


def shards(
    n_rows,
    stream,
    query,
    key,
    value,
    attn_gate,
    shift_mod,
    scale_mod,
    head_weight,
    head_bias,
    latent_mean,
    latent_std,
    conv_in_weight,
    conv_in_bias,
    norm_gain,
    conv_weight,
    conv_bias,
):
    width = query.shape[-1]
    flat = (FR, COLS, width)
    hbm = pl.BlockSpec(memory_space=pltpu.HBM)
    dma = pltpu.SemaphoreType.DMA
    bf = jnp.bfloat16
    f32 = jnp.float32
    line = lambda x: x.reshape(-1, min(128, x.shape[0]))
    shape = jax.ShapeDtypeStruct
    return pl.pallas_call(
        functools.partial(attend_kernel, n_rows),
        out_shape=shape((FR, 2, 2 * COLS, C), bf),
        in_specs=[hbm] * 16,
        out_specs=hbm,
        scratch_shapes=[
            pltpu.VMEM((576, 2 * C), bf),
            pltpu.VMEM((9, 3 * C, C), bf),
            pltpu.VMEM((C // 128, 128), f32),
            pltpu.VMEM((C // 128, 128), f32),
            pltpu.VMEM((C // 128, 128), f32),
            pltpu.VMEM((TOK, width), bf),
            pltpu.VMEM((width // 128, 128), f32),
            pltpu.VMEM((width // 128, 128), f32),
            pltpu.VMEM((width // 128, 128), f32),
            pltpu.VMEM((4 * LAT, width), bf),
            pltpu.VMEM((1, 4 * LAT), f32),
            pltpu.VMEM((1, LAT), f32),
            pltpu.VMEM((1, LAT), f32),
            pltpu.VMEM((9, 3 * LAT, C), bf),
            dma((13,)),
            pltpu.VMEM((HPD, GROUP, FR, COLS, HD), bf),
            pltpu.VMEM((HPD, FR, ROWS_EXT, COLS, HD), bf),
            pltpu.VMEM((HPD, FR, ROWS_EXT, COLS, HD), bf),
            pltpu.VMEM((HPD, GROUP, TOK, HD), bf),
            pltpu.VMEM((HEADS, TOK, HD), bf),
            pltpu.VMEM((TOK, KEYS), f32),
            pltpu.VMEM((3, TOK, 128), bf),
            dma((3, HPD)),
            dma((3, HPD, 3)),
            dma((3, HPD, 3)),
            dma((2, HPD, 2)),
            dma((2, HPD, 2)),
            dma((2, HPD, 2, 2)),
            dma((2, HPD, 2, 2)),
            dma((HPD, 3)),
            dma((HPD, 3)),
            dma((2,)),
            dma((2,)),
            pltpu.VMEM((4, 4, 2 * COLS + TOK, C), bf),
            pltpu.VMEM((4 * TOK, C), f32),
            pltpu.VMEM((FR, 2, 3, 2 * COLS, 128), f32),
            pltpu.VMEM((FR, 2, 2 * COLS, C), bf),
            dma((FR,)),
        ],
        compiler_params=pltpu.CompilerParams(
            collective_id=0, has_side_effects=True, vmem_limit_bytes=LIMIT
        ),
        name="attend",
    )(
        stream.reshape(TOK, width),
        query.reshape(flat),
        key.reshape(flat),
        value.reshape(flat),
        line(attn_gate),
        line(shift_mod),
        line(scale_mod),
        head_weight.T,
        line(head_bias),
        line(latent_mean),
        line(latent_std),
        conv_in_weight.reshape(9, 3 * LAT, C),
        line(conv_in_bias),
        line(norm_gain),
        line(conv_bias),
        conv_weight.reshape(9, 3 * C, C),
    )


def solution(mesh):
    cut = P("video", "row", None, None)
    part = P("video")
    return jax.shard_map(
        functools.partial(shards, mesh.shape["row"]),
        mesh=mesh,
        in_specs=(cut,) * 4 + (part,) * 3 + (P(),) * 9,
        out_specs=cut,
        check_vma=False,
    )
```

```python
import functools

import jax
import jax.numpy as jnp
from jax import lax
from jax.experimental import pallas as pl
from jax.experimental.pallas import tpu as pltpu
from jax.sharding import PartitionSpec as P

HEADS = 12
LAT = 16
GROUP = 4
HPD = HEADS // GROUP
HD = 128
FR = 4
COLS = 32
TOK = FR * COLS
ROWS_EXT = GROUP + 6
KEYS = FR * 7 * COLS
C = 384
NEG = -1e30
LIMIT = 62 << 20


def lanes(ref):
    return jnp.concatenate([ref[i : i + 1] for i in range(ref.shape[0])], axis=-1)


def attend_kernel(
    n_rows,
    stream_hbm,
    q_ref,
    k_ref,
    v_ref,
    gate_hbm,
    shift_hbm,
    scale_hbm,
    hw_hbm,
    hb_hbm,
    mean_hbm,
    std_hbm,
    cw_hbm,
    cib_hbm,
    gain_hbm,
    cb_hbm,
    w_hbm,
    out_hbm,
    w4_ref,
    w_ref,
    cib_ref,
    gain_ref,
    cb_ref,
    stream_ref,
    gate_ref,
    shift_ref,
    scale_ref,
    hw_ref,
    hb_ref,
    mean_ref,
    std_ref,
    cw_ref,
    load_sem,
    qb,
    kb,
    vb,
    ob,
    attn,
    bias,
    gbuf,
    own_sem,
    s1,
    r1,
    s2,
    r2,
    s5,
    r5,
    s3,
    r3,
    s4,
    r4,
    var,
    acc,
    wide,
    done,
    out_sem,
):
    row = lax.axis_index("row")
    g = row // GROUP
    j = row % GROUP
    groups = n_rows // GROUP
    half = j // 2
    mate = j + 1 - 2 * (j % 2)
    has_up = g > 0
    has_down = g < groups - 1
    first = row == 0
    last = row == n_rows - 1

    def head_cols(p, h):
        return pl.ds(pl.multiple_of((p * HPD + h) * HD, HD), HD)

    srcs = (k_ref, v_ref, q_ref)

    def level_dst(x, h, idx):
        if x == 2:
            return qb.at[h, idx]
        return (kb, vb)[x].at[h, :, idx + 3]

    own = []
    for h in range(HPD):
        for x in range(3):
            cp = pltpu.make_async_copy(
                srcs[x].at[:, :, head_cols(j, h)], level_dst(x, h, j), own_sem.at[x, h]
            )
            cp.start()
            own.append(cp)

    barrier = pltpu.get_barrier_semaphore()
    for d in range(1, GROUP):
        pl.semaphore_signal(barrier, inc=1, device_id={"row": g * GROUP + (j + d) % GROUP})

    @pl.when(has_up)
    def _():
        for p in (j, mate):
            pl.semaphore_signal(barrier, inc=1, device_id={"row": (g - 1) * GROUP + p})

    @pl.when(has_down)
    def _():
        for p in (j, mate):
            pl.semaphore_signal(barrier, inc=1, device_id={"row": (g + 1) * GROUP + p})

    cross_up = jnp.logical_and(j == 0, has_up)
    cross_down = jnp.logical_and(j == GROUP - 1, has_down)

    @pl.when(cross_up)
    def _():
        pl.semaphore_signal(barrier, inc=1, device_id={"row": row - 1})

    @pl.when(cross_down)
    def _():
        pl.semaphore_signal(barrier, inc=1, device_id={"row": row + 1})

    one = jnp.int32(1)
    zero = jnp.int32(0)
    expected = (
        3
        + 2 * jnp.where(has_up, one, zero)
        + 2 * jnp.where(has_down, one, zero)
        + jnp.where(cross_up, one, zero)
        + jnp.where(cross_down, one, zero)
    )
    pl.semaphore_wait(barrier, expected)

    def level_copy(x, h, d):
        p = (j + d) % GROUP
        return pltpu.make_async_remote_copy(
            src_ref=srcs[x].at[:, :, head_cols(p, h)],
            dst_ref=level_dst(x, h, j),
            send_sem=s1.at[x, h, d - 1],
            recv_sem=r1.at[x, h, d - 1],
            device_id={"row": g * GROUP + p},
        )

    def relay_copy(x, h, two):
        buf = (kb, vb)[x]
        if two:
            src, dst = buf.at[h, :, pl.ds(5 - 2 * half, 2)], buf.at[h, :, pl.ds(1 + 6 * half, 2)]
            dev = row + GROUP - 2 * GROUP * half
        else:
            src, dst = buf.at[h, :, pl.ds(5 - half, 1)], buf.at[h, :, pl.ds(9 - 9 * half, 1)]
            dev = row - GROUP + 2 * GROUP * half
        way = 0 if two else 1
        return pltpu.make_async_remote_copy(
            src_ref=src,
            dst_ref=dst,
            send_sem=s2.at[x, h, way],
            recv_sem=r2.at[x, h, way],
            device_id={"row": dev},
        )

    ahead = jnp.logical_or(
        jnp.logical_and(half == 0, has_down), jnp.logical_and(half == 1, has_up)
    )
    behind = jnp.logical_or(
        jnp.logical_and(half == 0, has_up), jnp.logical_and(half == 1, has_down)
    )

    def straight_copy(x, h, up, c, at):
        p = (j, mate)[c]
        way = 0 if up else 1
        return pltpu.make_async_remote_copy(
            src_ref=srcs[x].at[:, :, head_cols(p, h)],
            dst_ref=(kb, vb)[x].at[h, :, at],
            send_sem=s5.at[x, h, way, c],
            recv_sem=r5.at[x, h, way, c],
            device_id={"row": (g - 1 if up else g + 1) * GROUP + p},
        )

    send_up = jnp.logical_and(has_up, j <= 2)
    send_down = jnp.logical_and(has_down, j >= 1)
    recv_up = [jnp.logical_and(has_down, p <= 2) for p in (j, mate)]
    recv_down = [jnp.logical_and(has_up, p >= 1) for p in (j, mate)]

    for h in range(HPD):
        for x in range(2):
            for d in (2, 1, 3):
                level_copy(x, h, d).start()

        @pl.when(send_up)
        def _():
            for x in range(2):
                for c in range(2):
                    straight_copy(x, h, True, c, 7 + j).start()

        @pl.when(send_down)
        def _():
            for x in range(2):
                for c in range(2):
                    straight_copy(x, h, False, c, j - 1).start()

    for h in range(HPD):
        for d in (2, 1, 3):
            level_copy(2, h, d).start()

    pairs = (
        (stream_hbm, stream_ref),
        (gate_hbm, gate_ref),
        (shift_hbm, shift_ref),
        (scale_hbm, scale_ref),
        (hw_hbm, hw_ref),
        (hb_hbm, hb_ref),
        (mean_hbm, mean_ref),
        (std_hbm, std_ref),
        (cw_hbm, cw_ref),
        (cib_hbm, cib_ref),
        (gain_hbm, gain_ref),
        (cb_hbm, cb_ref),
        (w_hbm, w_ref),
    )
    loads = [
        pltpu.make_async_copy(src, dst, load_sem.at[i]) for i, (src, dst) in enumerate(pairs)
    ]
    for cp in loads:
        cp.start()

    tok_i = lax.broadcasted_iota(jnp.int32, (TOK, KEYS), 0)
    key_i = lax.broadcasted_iota(jnp.int32, (TOK, KEYS), 1)
    t = tok_i >> 5
    w = tok_i & 31
    span = 7 * COLS
    f = (
        jnp.where(key_i >= span, 1, 0)
        + jnp.where(key_i >= 2 * span, 1, 0)
        + jnp.where(key_i >= 3 * span, 1, 0)
    )
    fs = jnp.clip(t - 1, 0, FR - 3)
    cs = jnp.clip(w - 3, 0, COLS - 7)
    vcol = key_i & 31
    ok = (f >= fs) & (f < fs + 3) & (vcol >= cs) & (vcol < cs + 7)
    bias[...] = jnp.where(ok, 0.0, NEG)

    empty = jnp.zeros((HPD, FR, 3, COLS, HD), jnp.bfloat16)

    @pl.when(jnp.logical_not(has_up))
    def _():
        kb[:, :, 0:3] = empty
        vb[:, :, 0:3] = empty

    @pl.when(jnp.logical_not(has_down))
    def _():
        kb[:, :, 7:10] = empty
        vb[:, :, 7:10] = empty

    @pl.when(first)
    def _():
        gbuf[0] = jnp.zeros((TOK, 128), jnp.bfloat16)

    @pl.when(last)
    def _():
        gbuf[2] = jnp.zeros((TOK, 128), jnp.bfloat16)

    for cp in own:
        cp.wait()

    for h in range(HPD):
        for x in range(2):
            for d in range(1, GROUP):
                level_copy(x, h, d).wait_recv()

            @pl.when(ahead)
            def _():
                relay_copy(x, h, True).start()

            @pl.when(behind)
            def _():
                relay_copy(x, h, False).start()

    for cp in loads[:-1]:
        cp.wait()

    w4_ref[...] = jnp.zeros(w4_ref.shape, jnp.bfloat16)
    for ab in range(9):
        w4_ref[ab * 64 : ab * 64 + 48, 0:C] = cw_ref[ab]
        w4_ref[ab * 64 + 16 : ab * 64 + 64, C : 2 * C] = cw_ref[ab]

    key_row = lax.broadcasted_iota(jnp.int32, (1, KEYS), 1)
    fr = (
        jnp.where(key_row >= span, 1, 0)
        + jnp.where(key_row >= 2 * span, 1, 0)
        + jnp.where(key_row >= 3 * span, 1, 0)
    )
    rel_row = (key_row >> 5) - 7 * fr + (GROUP * g - 3)

    def out_copy(h, d):
        p = (j + d) % GROUP
        return pltpu.make_async_remote_copy(
            src_ref=ob.at[h, p],
            dst_ref=attn.at[j * HPD + h],
            send_sem=s3.at[h, d - 1],
            recv_sem=r3.at[h, d - 1],
            device_id={"row": g * GROUP + p},
        )

    for h in range(HPD):
        for d in range(1, GROUP):
            level_copy(2, h, d).wait_recv()
        for x in range(2):

            @pl.when(behind)
            def _():
                relay_copy(x, h, True).wait_recv()

            @pl.when(ahead)
            def _():
                relay_copy(x, h, False).wait_recv()

            for c in range(2):

                @pl.when(recv_up[c])
                def _():
                    straight_copy(x, h, True, c, 7).wait_recv()

                @pl.when(recv_down[c])
                def _():
                    straight_copy(x, h, False, c, 0).wait_recv()

        def one_row(i):
            qm = qb[h, i].reshape(TOK, HD)
            km = kb[h, :, pl.ds(i, 7)].reshape(KEYS, HD)
            vm = vb[h, :, pl.ds(i, 7)].reshape(KEYS, HD)
            s = lax.dot_general(
                qm, km, (((1,), (1,)), ((), ())), preferred_element_type=jnp.float32
            )
            src_row = rel_row + i
            row_bias = jnp.where((src_row >= 0) & (src_row < n_rows), 0.0, NEG)
            s = s * (HD**-0.5) + (bias[...] + row_bias)
            m = jnp.max(s, axis=1, keepdims=True)
            e = jnp.exp(s - m)
            l = jnp.sum(e, axis=1, keepdims=True)
            pr = (e * (1.0 / l)).astype(jnp.bfloat16)
            o = jnp.dot(pr, vm, preferred_element_type=jnp.float32)
            return o.astype(jnp.bfloat16)

        for d in (2, 1, 3):
            i = (j + d) % GROUP
            ob[h, i] = one_row(i)
            out_copy(h, d).start()
        attn[j * HPD + h] = one_row(j)

    for h in range(HPD):
        for d in range(1, GROUP):
            out_copy(h, d).wait_recv()

    attn_all = jnp.concatenate([attn[c] for c in range(HEADS)], axis=-1)
    resid = stream_ref[...].astype(jnp.float32) + lanes(gate_ref) * attn_all.astype(jnp.float32)
    center = resid - jnp.mean(resid, axis=-1, keepdims=True)
    spread = jnp.mean(center * center, axis=-1, keepdims=True)
    normed = center * lax.rsqrt(spread + 1e-06) * (1.0 + lanes(scale_ref)) + lanes(shift_ref)
    patch = lax.dot_general(
        normed.astype(jnp.bfloat16),
        hw_ref[...],
        (((1,), (1,)), ((), ())),
        preferred_element_type=jnp.float32,
    )
    patch = patch + hb_ref[...]
    std = jnp.concatenate([std_ref[...]] * 4, axis=-1)
    mean = jnp.concatenate([mean_ref[...]] * 4, axis=-1)
    latent = (patch * std + mean).astype(jnp.bfloat16)

    dst_l = lax.broadcasted_iota(jnp.int32, (4 * LAT, 128), 1)
    src_l = lax.broadcasted_iota(jnp.int32, (4 * LAT, 128), 0)
    part = (dst_l >> 4) & 3
    want = ((dst_l >> 6) * 2 + (1 - (part & 1))) * LAT + (dst_l & 15)
    pick = jnp.where(src_l == want, 1.0, 0.0).astype(jnp.bfloat16)
    spreadout = jnp.dot(latent, pick, preferred_element_type=jnp.float32)
    lane = lax.broadcasted_iota(jnp.int32, (TOK, 128), 1)
    col = lax.broadcasted_iota(jnp.int32, (TOK, 128), 0) & 31
    lane_part = (lane >> 4) & 3
    before = jnp.where(col == 0, 0.0, pltpu.roll(spreadout, 1, 0))
    after = jnp.where(col == COLS - 1, 0.0, pltpu.roll(spreadout, TOK - 1, 0))
    cells = jnp.where(lane_part == 0, before, jnp.where(lane_part == 3, after, spreadout))
    gbuf[1] = cells.astype(jnp.bfloat16)

    def latent_copy(up):
        way = 0 if up else 1
        return pltpu.make_async_remote_copy(
            src_ref=gbuf.at[1],
            dst_ref=gbuf.at[2 if up else 0],
            send_sem=s4.at[way],
            recv_sem=r4.at[way],
            device_id={"row": row - 1 if up else row + 1},
        )

    @pl.when(jnp.logical_not(first))
    def _():
        latent_copy(True).start()

    @pl.when(jnp.logical_not(last))
    def _():
        latent_copy(False).start()

    for h in range(HPD):
        for x in range(3):
            for d in range(1, GROUP):
                level_copy(x, h, d).wait_send()
        for x in range(2):

            @pl.when(ahead)
            def _():
                relay_copy(x, h, True).wait_send()

            @pl.when(behind)
            def _():
                relay_copy(x, h, False).wait_send()

            @pl.when(send_up)
            def _():
                for c in range(2):
                    straight_copy(x, h, True, c, 7).wait_send()

            @pl.when(send_down)
            def _():
                for c in range(2):
                    straight_copy(x, h, False, c, 0).wait_send()

        for d in range(1, GROUP):
            out_copy(h, d).wait_send()

    @pl.when(jnp.logical_not(first))
    def _():
        latent_copy(True).wait_send()
        latent_copy(False).wait_recv()

    @pl.when(jnp.logical_not(last))
    def _():
        latent_copy(False).wait_send()
        latent_copy(True).wait_recv()

    loads[-1].wait()
    decode(
        row, n_rows, gbuf, w4_ref, w_ref, cib_ref, gain_ref, cb_ref, out_hbm, var, acc, wide, done,
        out_sem,
    )


def decode(
    row, n_rows, cells_ref, w4_ref, w_ref, cib_ref, gain_ref, cb_ref, out_hbm, var, acc, wide, done,
    sem,
):
    six = jnp.concatenate([cells_ref[i] for i in range(3)], axis=-1)
    col = lax.broadcasted_iota(jnp.int32, (TOK, C), 0) & 31
    zeros = jnp.zeros((2 * COLS, C), jnp.bfloat16)
    pad = jnp.zeros((2 * COLS, 192), jnp.bfloat16)
    for y in range(4):
        rows3 = six[:, y * 64 : y * 64 + 192]
        padded = jnp.concatenate([pad, rows3], axis=0)
        x = jnp.concatenate([padded[i * COLS : i * COLS + TOK] for i in range(3)], axis=-1)
        h = jnp.dot(x, w4_ref[...], preferred_element_type=jnp.float32)
        acts = []
        for q in range(2):
            hidden = (h[:, q * C : (q + 1) * C] + lanes(cib_ref)).astype(jnp.bfloat16)
            hidden = hidden.astype(jnp.float32)
            if y in (1, 2):
                at = ((y - 1) * 2 + q) * TOK
                acc[at : at + TOK, :] = hidden + lanes(cb_ref)
            ms = jnp.mean(hidden * hidden, axis=-1, keepdims=True)
            scaled = hidden * lax.rsqrt(ms + 1e-06) * lanes(gain_ref)
            act = scaled / (1.0 + jnp.exp(-scaled))
            if y == 0:
                act = jnp.where(row > 0, act, 0.0)
            if y == 3:
                act = jnp.where(row < n_rows - 1, act, 0.0)
            acts.append(act)
        before = jnp.where(col == 0, 0.0, pltpu.roll(acts[1], 1, 0))
        after = jnp.where(col == COLS - 1, 0.0, pltpu.roll(acts[0], TOK - 1, 0))
        for i, piece in enumerate((before, acts[0], acts[1], after)):
            var[i, y, 0 : 2 * COLS] = zeros
            var[i, y, 2 * COLS :] = piece.astype(jnp.bfloat16)

    for a in range(3):
        for b in range(3):
            phases = []
            for y in range(2):
                taps = [var[i, y + b, a * COLS : a * COLS + TOK] for i in range(4)]
                for q in range(2):
                    phases.append(jnp.concatenate(taps[q : q + 3], axis=-1))
            lhs = jnp.concatenate(phases, axis=0)
            acc[...] += jnp.dot(lhs, w_ref[a * 3 + b], preferred_element_type=jnp.float32)

    copies = []
    for t in range(FR):
        for y in range(2):
            for q in range(2):
                at = (y * 2 + q) * TOK + t * COLS
                for c in range(3):
                    wide[t, y, c, pl.ds(q, COLS, stride=2), :] = acc[
                        at : at + COLS, c * 128 : (c + 1) * 128
                    ]
        for c in range(3):
            done[t, :, :, c * 128 : (c + 1) * 128] = wide[t, :, c].astype(jnp.bfloat16)
        cp = pltpu.make_async_copy(done.at[t], out_hbm.at[t], sem.at[t])
        cp.start()
        copies.append(cp)
    for cp in copies:
        cp.wait()


def shards(
    n_rows,
    stream,
    query,
    key,
    value,
    attn_gate,
    shift_mod,
    scale_mod,
    head_weight,
    head_bias,
    latent_mean,
    latent_std,
    conv_in_weight,
    conv_in_bias,
    norm_gain,
    conv_weight,
    conv_bias,
):
    width = query.shape[-1]
    flat = (FR, COLS, width)
    hbm = pl.BlockSpec(memory_space=pltpu.HBM)
    dma = pltpu.SemaphoreType.DMA
    bf = jnp.bfloat16
    f32 = jnp.float32
    line = lambda x: x.reshape(-1, min(128, x.shape[0]))
    shape = jax.ShapeDtypeStruct
    return pl.pallas_call(
        functools.partial(attend_kernel, n_rows),
        out_shape=shape((FR, 2, 2 * COLS, C), bf),
        in_specs=[hbm] * 16,
        out_specs=hbm,
        scratch_shapes=[
            pltpu.VMEM((576, 2 * C), bf),
            pltpu.VMEM((9, 3 * C, C), bf),
            pltpu.VMEM((C // 128, 128), f32),
            pltpu.VMEM((C // 128, 128), f32),
            pltpu.VMEM((C // 128, 128), f32),
            pltpu.VMEM((TOK, width), bf),
            pltpu.VMEM((width // 128, 128), f32),
            pltpu.VMEM((width // 128, 128), f32),
            pltpu.VMEM((width // 128, 128), f32),
            pltpu.VMEM((4 * LAT, width), bf),
            pltpu.VMEM((1, 4 * LAT), f32),
            pltpu.VMEM((1, LAT), f32),
            pltpu.VMEM((1, LAT), f32),
            pltpu.VMEM((9, 3 * LAT, C), bf),
            dma((13,)),
            pltpu.VMEM((HPD, GROUP, FR, COLS, HD), bf),
            pltpu.VMEM((HPD, FR, ROWS_EXT, COLS, HD), bf),
            pltpu.VMEM((HPD, FR, ROWS_EXT, COLS, HD), bf),
            pltpu.VMEM((HPD, GROUP, TOK, HD), bf),
            pltpu.VMEM((HEADS, TOK, HD), bf),
            pltpu.VMEM((TOK, KEYS), f32),
            pltpu.VMEM((3, TOK, 128), bf),
            dma((3, HPD)),
            dma((3, HPD, 3)),
            dma((3, HPD, 3)),
            dma((2, HPD, 2)),
            dma((2, HPD, 2)),
            dma((2, HPD, 2, 2)),
            dma((2, HPD, 2, 2)),
            dma((HPD, 3)),
            dma((HPD, 3)),
            dma((2,)),
            dma((2,)),
            pltpu.VMEM((4, 4, 2 * COLS + TOK, C), bf),
            pltpu.VMEM((4 * TOK, C), f32),
            pltpu.VMEM((FR, 2, 3, 2 * COLS, 128), f32),
            pltpu.VMEM((FR, 2, 2 * COLS, C), bf),
            dma((FR,)),
        ],
        compiler_params=pltpu.CompilerParams(
            collective_id=0, has_side_effects=True, vmem_limit_bytes=LIMIT
        ),
        name="attend",
    )(
        stream.reshape(TOK, width),
        query.reshape(flat),
        key.reshape(flat),
        value.reshape(flat),
        line(attn_gate),
        line(shift_mod),
        line(scale_mod),
        head_weight.T,
        line(head_bias),
        line(latent_mean),
        line(latent_std),
        conv_in_weight.reshape(9, 3 * LAT, C),
        line(conv_in_bias),
        line(norm_gain),
        line(conv_bias),
        conv_weight.reshape(9, 3 * C, C),
    )


def solution(mesh):
    cut = P("video", "row", None, None)
    part = P("video")
    return jax.shard_map(
        functools.partial(shards, mesh.shape["row"]),
        mesh=mesh,
        in_specs=(cut,) * 4 + (part,) * 3 + (P(),) * 9,
        out_specs=cut,
        check_vma=False,
    )
```
